32 devices in a mesh: row: 4 (over y, core), col: 4 (over z), layer: 2 (over x).
Axes of the slice: x: 2, y: 2, z: 4, core: 2. Of those that a mesh axis runs over, the one named last changes fastest.
Arguments:
- a_tiles: float32 [16, 8, 128, 128], P('row', ('col', 'layer')), may hold values from -2 to 2
- a_cols: int32 [16, 8], P('row', ('col', 'layer')), may hold values from 0 to 15, as said below
- out_cols: int32 [16, 8], P('row', ('col', 'layer')), may hold values from 0 to 15, as said below
Outputs:
- squared: float32 [16, 8, 128, 128], P('row', ('col', 'layer'))
The draws below stay inside these ranges and needn't reach their ends.
Inputs may be any that keep to these rules, and one draw needn't show every extreme that they name: `a_cols`: slot s of every tile row names a column j with j // 8 == s % 2 and j % 4 == s // 2. `out_cols`: slot s of every tile row names a column j with j // 8 == s % 2 and j % 4 == s // 2.
All inputs are finite; a program needn't handle non-finite values.
Results may differ from the reference program's by a relative error of at most 0.0003.
Values sent between devices are 32-bit elements; how exact they have to be, the bound alone decides.
No kernel may reach another device: no remote copies, remote signals or barrier semaphores. Data moves between devices by JAX's collectives and lax.ppermute only.
A program may use at most 64 MiB of HBM per device.

```python
import jax
import jax.numpy as jnp
from jax import lax

TILE = 128
NTILE = 16
INNER = 8
SPAN = 2
SLOTS = 8
N_COL = 4
N_LAYER = 2


def cell_columns(key):
    slot_index = jnp.arange(SLOTS, dtype=jnp.int32)
    cell_column = slot_index // N_LAYER
    cell_layer = slot_index % N_LAYER
    offsets = jax.random.randint(key, (NTILE, SLOTS), 0, SPAN, dtype=jnp.int32)
    return (cell_layer[None, :] * INNER + offsets * N_COL + cell_column[None, :]).astype(jnp.int32)


def draw_a_cols(key, part):
    return cell_columns(jax.random.fold_in(key, 11))


def draw_out_cols(key, part):
    return cell_columns(jax.random.fold_in(key, 23))


def block_levels(own_key, dims, shards, least, high):
    gain, own = 1.0, jax.random.fold_in(own_key, 6)
    for axis_at, blocks in shards:
        heights = jnp.exp(jax.random.uniform(jax.random.fold_in(own, axis_at), (blocks,), jnp.float32, least / len(shards), high / len(shards)))
        gain = gain * jnp.repeat(heights, dims[axis_at] // blocks).reshape([-1 if axis == axis_at else 1 for axis in range(len(dims))])
    return gain


def bell_draw(rng, extent, spread, reach, cuts=(), kind=jnp.bfloat16):
    entries = spread * jax.random.normal(rng, extent, jnp.float32)
    if cuts:
        entries = entries * block_levels(rng, extent, cuts, -0.22, 0.18)
    return jnp.clip(entries, -reach, reach).astype(kind)


def setup_inputs(seed: int = 0) -> dict:
    key_of = jax.random.split(jax.random.key(seed), 4)
    a_tiles = bell_draw(key_of[0], (NTILE, SLOTS, TILE, TILE), 0.125, 2.0, ((0, 4), (1, 8)), jnp.float32)
    a_cols = draw_a_cols(jax.random.fold_in(key_of[3], 71), 0)
    out_cols = draw_out_cols(jax.random.fold_in(key_of[3], 71), 0)
    return dict(a_tiles=a_tiles, a_cols=a_cols, out_cols=out_cols)


def reference(a_tiles, a_cols, out_cols):
    def one_row(packed):
        row_tiles, row_cols, row_wanted = packed
        partner_tiles = a_tiles[row_cols]
        partner_cols = a_cols[row_cols]
        matches = partner_cols == row_wanted[None, :]
        selected = jnp.where(matches[:, :, None, None], partner_tiles, jnp.zeros((), partner_tiles.dtype))
        return jnp.einsum("sab,smbc->mac", row_tiles, selected, precision=lax.Precision.HIGHEST)

    return lax.map(one_row, (a_tiles, a_cols, out_cols))
```

```python
import functools

import jax
import jax.numpy as jnp
from jax import lax
from jax.experimental import pallas as pl
from jax.experimental.pallas import tpu as pltpu
from jax.sharding import PartitionSpec as P


PAD = 8
VMEM = pl.BlockSpec(memory_space=pltpu.VMEM)
SMEM = pl.BlockSpec(memory_space=pltpu.SMEM)


def swap(value, axis, distance):
    count = lax.axis_size(axis)
    return lax.ppermute(value, axis, [(i, i ^ distance) for i in range(count)])


def pack_kernel(cols_ref, tiles_ref, packed_ref):
    rows = tiles_ref.shape[0]
    packed_ref[pl.ds(0, rows), :] = tiles_ref[...]
    index = lax.broadcasted_iota(jnp.int32, (PAD, 128), 0)
    value = jnp.zeros((PAD, 128), jnp.float32)
    for row in range(cols_ref.shape[0]):
        value = jnp.where(index == row, cols_ref[row, 0].astype(jnp.float32), value)
    packed_ref[pl.ds(rows, PAD), :] = value


def split(value):
    high = value.astype(jnp.bfloat16)
    return high, (value - high.astype(jnp.float32)).astype(jnp.bfloat16)


def right_kernel(distances, rows_dev, tile, place_ref, *refs):
    blocks, (pair_ref, cols_ref) = refs[: len(distances)], refs[len(distances) :]
    for distance, block in zip(distances, blocks):
        first = (place_ref[0] ^ distance) * rows_dev
        for row in range(rows_dev):
            high, low = split(block[pl.ds(row * tile, tile), :])
            pair_ref[first + row, :, pl.ds(0, tile)] = high
            pair_ref[first + row, :, pl.ds(tile, tile)] = low
            cols_ref[first + row] = jnp.broadcast_to(
                block[pl.ds(rows_dev * tile + row, 1), :], (PAD, 128)
            )


def product_kernel(
    distances, rows_dev, tile, sizes, add, place_ref, wanted_ref, pair_ref, cols_ref, *refs
):
    inner_rows, col_count, cell_width = sizes
    blocks, out_ref = refs[: len(distances)], refs[-1]
    sums = [None] * rows_dev
    for at in range(0, len(distances), 2):
        part = list(zip(distances, blocks))[at : at + 2]
        for row in range(rows_dev):
            highs, lows, picks = [], [], []
            for (col_step, layer_step), block in part:
                base = (place_ref[2] ^ layer_step) * inner_rows + (place_ref[1] ^ col_step)
                column = block[pl.ds(rows_dev * tile + row, 1), :]
                picked = None
                for offset in range(cell_width):
                    source = base + offset * col_count
                    taken = (column == source.astype(jnp.float32)) & (
                        cols_ref[source, pl.ds(0, 1), :] == wanted_ref[row, 0].astype(jnp.float32)
                    )
                    weight = jnp.where(taken, 1.0, 0.0).astype(jnp.bfloat16)
                    weight = jnp.concatenate([weight, weight], axis=1)
                    term = pair_ref[source] * weight
                    picked = term if picked is None else picked + term
                high, low = split(block[pl.ds(row * tile, tile), :])
                highs.append(high)
                lows.append(low)
                picks.append(picked)
            high = jnp.concatenate(highs, axis=1)
            low = jnp.concatenate(lows, axis=1)
            pick = jnp.concatenate(picks, axis=0)
            both = jnp.dot(high, pick, preferred_element_type=jnp.float32)
            rest = jnp.dot(low, pick[:, :tile], preferred_element_type=jnp.float32)
            term = both[:, :tile] + (both[:, tile:] + rest)
            sums[row] = term if sums[row] is None else sums[row] + term
    for row in range(rows_dev):
        total = sums[row]
        if add:
            total = total + refs[-2][pl.ds(row * tile, tile), :]
        out_ref[pl.ds(row * tile, tile), :] = total


def gather_left(own, col_count, layer_count):
    left = {(0, 0): own}
    high = col_count // 2
    while high > 1:
        left[high, 0] = swap(own, "col", high)
        high //= 2
    for step in range(1, col_count):
        if (step, 0) not in left:
            bit = step & -step
            left[step, 0] = swap(left[step ^ bit, 0], "col", bit)
    for step in range(col_count):
        for layer_step in range(1, layer_count):
            left[step, layer_step] = swap(left[step, 0], "layer", layer_step)
    return left


def gather_right(own, row_count):
    right = {0: own}
    for step in range(2, row_count, 2):
        right[step] = swap(own, "row", step)
    for step in range(1, row_count, 2):
        right[step] = swap(right[step ^ 1], "row", 1)
    return right


def local(a_tiles, a_cols, out_cols):
    rows_dev, tile = a_tiles.shape[0], a_tiles.shape[2]
    row_count = lax.axis_size("row")
    col_count = lax.axis_size("col")
    layer_count = lax.axis_size("layer")
    rows_all = rows_dev * row_count
    inner_rows = rows_all // layer_count
    cell_width = inner_rows // col_count
    place = jnp.stack([lax.axis_index("row"), lax.axis_index("col"), lax.axis_index("layer")])
    own = pl.pallas_call(
        pack_kernel,
        out_shape=jax.ShapeDtypeStruct((rows_dev * tile + PAD, tile), jnp.float32),
        in_specs=[SMEM, VMEM],
        out_specs=VMEM,
    )(a_cols, a_tiles.reshape(rows_dev * tile, tile))
    left = gather_left(own, col_count, layer_count)
    right = gather_right(own, row_count)
    pair, cols = pl.pallas_call(
        functools.partial(right_kernel, tuple(right), rows_dev, tile),
        out_shape=(
            jax.ShapeDtypeStruct((rows_all, tile, 2 * tile), jnp.bfloat16),
            jax.ShapeDtypeStruct((rows_all, PAD, 128), jnp.float32),
        ),
        in_specs=[SMEM] + [VMEM] * len(right),
        out_specs=(VMEM, VMEM),
    )(place, *right.values())

    def product(steps, before):
        extra = [] if before is None else [before]
        return pl.pallas_call(
            functools.partial(
                product_kernel,
                steps,
                rows_dev,
                tile,
                (inner_rows, col_count, cell_width),
                before is not None,
            ),
            out_shape=jax.ShapeDtypeStruct((rows_dev * tile, tile), jnp.float32),
            in_specs=[SMEM, SMEM] + [VMEM] * (2 + len(steps) + len(extra)),
            out_specs=VMEM,
        )(place, out_cols, pair, cols, *[left[step] for step in steps], *extra)

    last = (col_count - 1, layer_count - 1)
    first = tuple(step for step in left if step != last)
    total = product((last,), product(first, None))
    return total.reshape(rows_dev, 1, tile, tile)


def solution(mesh):
    in_specs = (
        P("row", ("col", "layer"), None, None),
        P("row", ("col", "layer")),
        P("row", ("col", "layer")),
    )
    out_specs = P("row", ("col", "layer"), None, None)
    return jax.shard_map(local, mesh=mesh, in_specs=in_specs, out_specs=out_specs, check_vma=False)
```

```python
import functools

import jax
import jax.numpy as jnp
from jax import lax
from jax.experimental import pallas as pl
from jax.experimental.pallas import tpu as pltpu
from jax.sharding import PartitionSpec as P


PAD = 8
VMEM = pl.BlockSpec(memory_space=pltpu.VMEM)
SMEM = pl.BlockSpec(memory_space=pltpu.SMEM)
HBM = pl.BlockSpec(memory_space=pltpu.HBM)
PARAMS = pltpu.CompilerParams(vmem_limit_bytes=16 << 20)


def swap(value, axis, distance):
    count = lax.axis_size(axis)
    return lax.ppermute(value, axis, [(i, i ^ distance) for i in range(count)])


ACROSS = ((1, 1),)


def pack_kernel(cols_ref, tiles_ref, *refs):
    packed, (here, done) = refs[:-2], refs[-2:]
    rows, tile = tiles_ref.shape[0], tiles_ref.shape[1]
    cols = pltpu.make_async_copy(cols_ref, here, done.at[0])
    cols.start()
    copies, first = [], 0
    for at, ref in enumerate(packed):
        held = ref.shape[0] - PAD
        copy = pltpu.make_async_copy(
            tiles_ref.at[pl.ds(first, held)], ref.at[pl.ds(0, held)], done.at[1 + at]
        )
        copy.start()
        copies.append((first, held, copy))
        first = (first + held) % rows
    cols.wait()
    index = lax.broadcasted_iota(jnp.int32, (PAD, 128), 0)
    for ref, (first, held, _) in zip(packed, copies):
        value = jnp.zeros((PAD, 128), jnp.float32)
        for row in range(held // tile):
            column = here[first // tile + row].astype(jnp.float32)
            value = jnp.where(index == row, column, value)
        ref[pl.ds(held, PAD), :] = value
    for _, _, copy in copies:
        copy.wait()


def split(value):
    high = value.astype(jnp.bfloat16)
    return high, (value - high.astype(jnp.float32)).astype(jnp.bfloat16)


def right_kernel(distances, rows_dev, tile, *refs):
    blocks, (pair_ref, cols_ref) = refs[: len(distances)], refs[len(distances) :]
    for distance, block in zip(distances, blocks):
        first = (lax.axis_index("row") ^ distance) * rows_dev
        for row in range(rows_dev):
            high, low = split(block[pl.ds(row * tile, tile), :])
            pair_ref[first + row, :, pl.ds(0, tile)] = high
            pair_ref[first + row, :, pl.ds(tile, tile)] = low
            cols_ref[first + row] = jnp.broadcast_to(
                block[pl.ds(rows_dev * tile + row, 1), :], (PAD, 128)
            )


def product_kernel(pieces, rows_dev, tile, sizes, add, wanted_ref, pair_ref, cols_ref, *refs):
    inner_rows, col_count, cell_width = sizes
    blocks, out_ref = refs[: len(pieces)], refs[-1]
    col, layer = lax.axis_index("col"), lax.axis_index("layer")
    for row in range(rows_dev):
        terms = []
        for (first, col_step, layer_step), block in zip(pieces, blocks):
            held = (block.shape[0] - PAD) // tile
            if not first <= row < first + held:
                continue
            base = (layer ^ layer_step) * inner_rows + (col ^ col_step)
            column = block[pl.ds(held * tile + row - first, 1), :]
            picked = None
            for offset in range(cell_width):
                source = base + offset * col_count
                taken = (column == source.astype(jnp.float32)) & (
                    cols_ref[source, pl.ds(0, 1), :] == wanted_ref[row].astype(jnp.float32)
                )
                weight = jnp.where(taken, 1.0, 0.0).astype(jnp.bfloat16)
                weight = jnp.concatenate([weight, weight], axis=1)
                term = pair_ref[source] * weight
                picked = term if picked is None else picked + term
            terms.append((*split(block[pl.ds((row - first) * tile, tile), :]), picked))
        total = refs[-2][pl.ds(row * tile, tile), :] if add else None
        for at in range(0, len(terms), 2):
            highs, lows, picks = zip(*terms[at : at + 2])
            high = jnp.concatenate(highs, axis=1)
            low = jnp.concatenate(lows, axis=1)
            pick = jnp.concatenate(picks, axis=0)
            both = jnp.dot(high, pick, preferred_element_type=jnp.float32)
            rest = jnp.dot(low, pick[:, :tile], preferred_element_type=jnp.float32)
            term = both[:, :tile] + (both[:, tile:] + rest)
            total = term if total is None else total + term
        out_ref[pl.ds(row * tile, tile), :] = total


def compute(a_tiles, a_cols, out_cols):
    rows_dev, tile = a_tiles.shape[0], a_tiles.shape[2]
    row_count = lax.axis_size("row")
    col_count = lax.axis_size("col")
    layer_count = lax.axis_size("layer")
    rows_all = rows_dev * row_count
    inner_rows = rows_all // layer_count
    cell_width = inner_rows // col_count
    half = rows_dev // 2
    held = (rows_dev, half, rows_dev - half)
    own, *parts = pl.pallas_call(
        pack_kernel,
        out_shape=[jax.ShapeDtypeStruct((n * tile + PAD, tile), jnp.float32) for n in held],
        in_specs=[HBM, HBM],
        out_specs=[VMEM] * len(held),
        scratch_shapes=[
            pltpu.SMEM((rows_dev,), jnp.int32),
            pltpu.SemaphoreType.DMA((1 + len(held),)),
        ],
        compiler_params=PARAMS,
    )(a_cols.reshape(rows_dev), a_tiles.reshape(rows_dev * tile, tile))

    left = {}
    for part, value in enumerate(parts):
        left[part, 0, 0] = value
        step = col_count // 2
        while step >= 1:
            left[part, step, 0] = swap(value, "col", step)
            step //= 2
        for step in range(1, col_count):
            if (part, step, 0) not in left:
                bit = step & -step
                left[part, step, 0] = swap(left[part, step ^ bit, 0], "col", bit)
        for step in range(col_count):
            for layer_step in range(1, layer_count):
                if (part, step) in ACROSS:
                    value = left[part, 0, layer_step]
                    left[part, step, layer_step] = swap(value, "col", step)
                else:
                    value = left[part, step, 0]
                    left[part, step, layer_step] = swap(value, "layer", layer_step)
    right = {0: own}
    for step in range(2, row_count, 2):
        right[step] = swap(own, "row", step)
    for step in range(1, row_count, 2):
        right[step] = swap(right[step ^ 1], "row", 1)

    pair, cols = pl.pallas_call(
        functools.partial(right_kernel, tuple(right), rows_dev, tile),
        out_shape=(
            jax.ShapeDtypeStruct((rows_all, tile, 2 * tile), jnp.bfloat16),
            jax.ShapeDtypeStruct((rows_all, PAD, 128), jnp.float32),
        ),
        in_specs=[VMEM] * len(right),
        out_specs=(VMEM, VMEM),
        compiler_params=PARAMS,
    )(*right.values())
    wanted = out_cols.reshape(rows_dev)

    def product(pieces, before):
        extra = [] if before is None else [before]
        return pl.pallas_call(
            functools.partial(
                product_kernel,
                tuple((part * half, *steps) for part, *steps in pieces),
                rows_dev,
                tile,
                (inner_rows, col_count, cell_width),
                before is not None,
            ),
            out_shape=jax.ShapeDtypeStruct((rows_dev * tile, tile), jnp.float32),
            in_specs=[SMEM] + [VMEM] * (2 + len(pieces) + len(extra)),
            out_specs=VMEM,
            compiler_params=PARAMS,
        )(wanted, pair, cols, *[left[piece] for piece in pieces], *extra)

    last = [piece for piece in left if piece[1:] == (col_count - 1, layer_count - 1)]
    first = [piece for piece in left if piece not in last]
    total = product(last, product(first, None))
    return total.reshape(rows_dev, 1, tile, tile)


def solution(mesh):
    in_specs = (
        P("row", ("col", "layer"), None, None),
        P("row", ("col", "layer")),
        P("row", ("col", "layer")),
    )
    out_specs = P("row", ("col", "layer"), None, None)
    return jax.shard_map(compute, mesh=mesh, in_specs=in_specs, out_specs=out_specs, check_vma=False)
```
